128 devices in a mesh: gx: 8 (over z, core), gy: 16 (over y, x).
Axes of the slice: x: 4, y: 4, z: 4, core: 2. Of those that a mesh axis runs over, the one named last changes fastest.
Arguments:
- center_points: float32 [3, 8192], P(None, ('gx', 'gy')), may hold values from 0 to 1
- displacements: float32 [3, 8192], P(None, ('gx', 'gy')), may hold values from -24 to 24
- edge_points: float32 [3, 131072], P(None, ('gx', 'gy')), may hold values from 0 to 1
- send_list: int32 [128, 16, 3], P(('gx', 'gy')), may hold values from -1 to 15, as said below
- block_tiles: int32 [512, 12], P(('gx', 'gy')), may hold values from 0 to 47, as said below
- block_count: int32 [128], P(('gx', 'gy')), may hold values from 1 to 4, as said below
Outputs:
- coefficients: float32 [3, 8192], P(None, ('gx', 'gy'))
- block_motion: float32 [512, 3, 64, 4096], P(('gx', 'gy'))
The draws below stay inside these ranges and needn't reach their ends.
Inputs may be any that keep to these rules, and one draw needn't show every extreme that they name: `send_list`: A zone is the 16 devices that share a gx index. Entry [s, r, c] names the local edge that device s sends to device r of its zone in position c, or -1 where that position carries nothing. Every position that a live block slot names carries an edge. `block_tiles`: the entry for a block slot and edge is the position s * 3 + c, in the tiles that reach the block's device, of the tile sent by device s of its zone in position c; the 48 entries of one device are all distinct, so a device with 4 live blocks receives 3 tiles from every device of its zone. `block_count`: the live slots of a device are its first ones; in every zone some device holds 4 blocks.
All inputs are finite; a program needn't handle non-finite values.
Results may differ from the reference program's by a relative error of at most 0.0003.
Values sent between devices are 32-bit elements; how exact they have to be, the bound alone decides.
A program may use at most 128 MiB of HBM per device.

```python
import jax
import jax.numpy as jnp
from jax import lax

NC = 8192
S = 64
ITERS = 3
SLOTS = 4
EDGE_DEV = 16
CAP = 3
N_GX = 8
N_GY = 16


def layout_tables(key):
    zones = N_GX
    group_size = N_GY
    devices = N_GX * N_GY
    places = SLOTS * 12
    base_key = jax.random.fold_in(key, 4242)
    key_count, key_full, key_perm, key_edge = jax.random.split(base_key, 4)
    counts = jax.random.randint(key_count, (zones, group_size), 1, SLOTS + 1)
    fullest = jax.random.randint(key_full, (zones, 1), 0, group_size)
    counts = jnp.where(jnp.arange(group_size)[None, :] == fullest, SLOTS, counts).reshape(devices).astype(jnp.int32)
    orders = jax.vmap(lambda sub_key: jax.random.permutation(sub_key, places))(jax.random.split(key_perm, devices)).astype(jnp.int32)
    edge_ids = jax.random.randint(key_edge, (devices, places), 0, EDGE_DEV).astype(jnp.int32)
    alive_tile = jnp.arange(places)[None, :] // 12 < counts[:, None]
    inverse = jnp.argsort(orders, axis=1)
    wanted = jnp.where(jnp.take_along_axis(alive_tile, inverse, 1), jnp.take_along_axis(edge_ids, inverse, 1), -1)
    sends = wanted.reshape(zones, group_size, group_size, CAP).transpose(0, 2, 1, 3).reshape(devices, group_size, CAP)
    tiles_table = orders.reshape(devices * SLOTS, 12)
    return (counts, sends.astype(jnp.int32), tiles_table)


def draw_send_list(key, part):
    return layout_tables(key)[1]


def draw_block_tiles(key, part):
    return layout_tables(key)[2]


def draw_block_count(key, part):
    return layout_tables(key)[0]


def draw_displacements(key, part):
    base_key = jax.random.fold_in(key, 1717)
    key_base = jax.random.fold_in(base_key, 0)
    ramp = 1.0 + 2.0 * jnp.arange(NC).astype(jnp.float32) / (NC - 1)
    values = jnp.clip(jax.random.normal(key_base, (3, NC), jnp.float32), -8.0, 8.0) * ramp[None, :]
    return jnp.clip(values, -24.0, 24.0)


def steps_of(stream_key, shape, shards, low, largest):
    def one(axis_at, shards_of):
        steps = jax.random.uniform(jax.random.fold_in(jax.random.fold_in(stream_key, 6), axis_at), (shards_of,), jnp.float32, low / len(shards), largest / len(shards))
        return jnp.repeat(jnp.exp(steps), shape[axis_at] // shards_of).reshape((-1,) + (1,) * (len(shape) - axis_at - 1))

    loudness = one(*shards[0])
    for cut in shards[1:]:
        loudness = loudness * one(*cut)
    return loudness


def setup_inputs(seed: int = 0) -> dict:
    arg_keys = jax.random.split(jax.random.key(seed), 7)
    return {
        "center_points": jnp.clip(1.0 * jax.random.uniform(arg_keys[0], (3, NC), jnp.float32) ** steps_of(arg_keys[0], (3, NC), ((1, 128),), -0.2, 0.2), 0.0, 1.0),
        "displacements": draw_displacements(jax.random.fold_in(arg_keys[6], 71), 0),
        "edge_points": jnp.clip(1.0 * jax.random.uniform(arg_keys[2], (3, N_GX * N_GY * EDGE_DEV * S), jnp.float32) ** steps_of(arg_keys[2], (3, N_GX * N_GY * EDGE_DEV * S), ((1, 128),), -0.2, 0.2), 0.0, 1.0),
        "send_list": draw_send_list(jax.random.fold_in(arg_keys[6], 71), 0),
        "block_tiles": draw_block_tiles(jax.random.fold_in(arg_keys[6], 71), 0),
        "block_count": draw_block_count(jax.random.fold_in(arg_keys[6], 71), 0),
    }


RADIUS = 0.25
SHIFT = 0.1
HIGHEST_PREC = lax.Precision.HIGHEST

def pair_distance(left_points, right_points):
    squared = (left_points[0][:, None] - right_points[0][None, :]) ** 2
    squared = squared + (left_points[1][:, None] - right_points[1][None, :]) ** 2
    squared = squared + (left_points[2][:, None] - right_points[2][None, :]) ** 2
    return squared

def wendland(squared):
    radial = jnp.sqrt(squared) / RADIUS
    remain = jnp.maximum(1.0 - radial, 0.0)
    return remain ** 4 * (4.0 * radial + 1.0)

def transfinite(edge_tiles):
    extent = edge_tiles.shape[2]
    fraction = jnp.arange(extent).astype(jnp.float32) / (extent - 1)
    blends = jnp.stack([1.0 - fraction, fraction])
    pair_weight = (blends[None, :, :, None] * blends[:, None, None, :]).reshape(4, extent, extent)
    first_dir = edge_tiles[:, 0:4]
    second_dir = edge_tiles[:, 4:8]
    third_dir = edge_tiles[:, 8:12]
    straight = blends[0][None, None, :] * first_dir[:, :, 0:1] + blends[1][None, None, :] * first_dir[:, :, extent - 1:extent]
    result = jnp.einsum('cei,ejk->cijk', first_dir - 2.0 * straight, pair_weight, precision=HIGHEST_PREC)
    result = result + jnp.einsum('cej,eik->cijk', second_dir, pair_weight, precision=HIGHEST_PREC)
    result = result + jnp.einsum('cek,eij->cijk', third_dir, pair_weight, precision=HIGHEST_PREC)
    return result.reshape(3, extent, extent * extent)

def conjugate(right_side, matvec, global_sum):
    norm_start = global_sum(lax.optimization_barrier(jnp.sum(right_side * right_side, axis=1, keepdims=True)))

    def cg_turn(iteration, cg_state):
        iterate, remain, search, norm_now = cg_state
        applied = matvec(search)
        step_size = norm_now / global_sum(lax.optimization_barrier(jnp.sum(search * applied, axis=1, keepdims=True)))
        iterate = iterate + step_size * search
        remain = remain - step_size * applied
        norm_next = global_sum(lax.optimization_barrier(jnp.sum(remain * remain, axis=1, keepdims=True)))
        search = remain + norm_next / norm_now * search
        return (iterate, remain, search, norm_next)
    cg_state = lax.fori_loop(0, ITERS, cg_turn, (jnp.zeros_like(right_side), right_side, right_side, norm_start))
    return cg_state[0]

def reference(center_points, displacements, edge_points, send_list, block_tiles, block_count):
    kernel = wendland(pair_distance(center_points, center_points))

    def matvec(search):
        return jnp.dot(search, kernel, precision=HIGHEST_PREC) + SHIFT * search

    def global_sum(partial_value):
        return partial_value
    coefficients = conjugate(displacements, matvec, global_sum)
    devices = N_GX * N_GY
    owned_points = edge_points.reshape(3, devices, EDGE_DEV * S).transpose(1, 0, 2)

    def evaluate(points):
        weights = wendland(pair_distance(points, center_points))
        return jnp.dot(coefficients, weights.T, precision=HIGHEST_PREC)
    motion = lax.map(evaluate, owned_points).reshape(devices, 3, EDGE_DEV, S)
    holder = (jnp.arange(devices * SLOTS) // SLOTS).astype(jnp.int32)
    source = holder[:, None] // N_GY * N_GY + block_tiles // CAP
    receiver = (holder[:, None] % N_GY).astype(jnp.int32)
    column = block_tiles % CAP
    local_edge = jnp.maximum(send_list[source, receiver, column], 0)
    gathered = motion[source, :, local_edge, :].transpose(0, 2, 1, 3)
    alive_slot = jnp.arange(devices * SLOTS).astype(jnp.int32) % SLOTS < block_count[holder]

    def fill_block(element):
        edge_tiles, is_alive = element
        return jnp.where(is_alive, transfinite(edge_tiles), 0.0)
    block_motion = lax.map(fill_block, (gathered, alive_slot))
    return (coefficients, block_motion)
```

```python
import jax
import jax.numpy as jnp
from jax import lax
from jax.experimental import pallas as pl
from jax.experimental.pallas import tpu as pltpu
from jax.sharding import PartitionSpec as P

MESH = pl.DeviceIdType.MESH
F32 = jnp.float32
BF16 = jnp.bfloat16

NC = 8192
S = 64
SLOTS = 4
EDGE_DEV = 16
CAP = 3
N_GX = 8
N_GY = 16
CHIPS = 64
POINTS = EDGE_DEV * S
SHIFT = 0.1
CHUNK = 256
NCHUNK = NC // CHUNK
RING = (0, 1, 2, 1)
OFFSETS = sorted(
    [(a, b, c) for a in range(4) for b in range(4) for c in range(4) if (a, b, c) != (0, 0, 0)],
    key=lambda o: -sum(RING[q] for q in o),
)


def dot_nn(left, right):
    return lax.dot_general(left, right, (((1,), (0,)), ((), ())), preferred_element_type=F32)


def dot_nt(left, right):
    return lax.dot_general(left, right, (((1,), (1,)), ((), ())), preferred_element_type=F32)


def bump(squared):
    squared = jnp.maximum(squared, 1e-30)
    root = squared * lax.rsqrt(squared)
    t = jnp.maximum(4.0 - root, 0.0)
    t2 = t * t
    return (t2 * t2) * (5.0 - t)


def halves(v):
    high = v.astype(BF16)
    return high, (v - high.astype(F32)).astype(BF16)


def parts(v):
    high = v.astype(BF16).astype(F32)
    rest = v - high
    mid = rest.astype(BF16).astype(F32)
    return high, mid, rest - mid


def rows8(shape):
    return lax.broadcasted_iota(jnp.int32, shape, 0)


def left_stack(x8):
    row = rows8(x8.shape)
    norm = jnp.sum(x8 * x8, axis=0, keepdims=True)
    v = jnp.where(row < 3, -2.0 * x8, jnp.where(row == 3, 1.0, jnp.where(row == 4, norm, 0.0)))
    h, m, l = parts(v)
    return jnp.concatenate([h, h, m, m, h, l, jnp.zeros_like(h), jnp.zeros_like(h)], axis=0)


def right_stack(x8):
    row = rows8(x8.shape)
    norm = jnp.sum(x8 * x8, axis=0, keepdims=True)
    v = jnp.where(row < 3, x8, jnp.where(row == 3, norm, jnp.where(row == 4, 1.0, 0.0)))
    h, m, l = parts(v)
    return jnp.concatenate([h, m, h, m, l, h, jnp.zeros_like(h), jnp.zeros_like(h)], axis=0)


def motion_kernel(
    cen_ref, dis_ref, pts_ref, list_ref, coef_ref, tile_ref,
    half, cbuf, g1, g2, g3, right, left, kh, kl, ph, plo, sf, sp,
    d_ref, x_ref, r_ref, s_ref, motion, outbox, inbox, p8, ssem, rsem,
):
    gx = lax.axis_index("gx")
    gy = lax.axis_index("gy")
    z = lax.div(gx, 2)
    core = lax.rem(gx, 2)
    y = lax.div(gy, 4)
    x = lax.rem(gy, 4)
    me = z * N_GY + gy

    barrier = pltpu.get_barrier_semaphore()
    for k in range(1, N_GY):
        pl.semaphore_signal(
            barrier, inc=1, device_id=(gx, lax.rem(gy + k, N_GY)), device_id_type=MESH
        )
    for k in range(1, N_GX):
        pl.semaphore_signal(
            barrier, inc=1, device_id=(lax.rem(gx + k, N_GX), gy), device_id_type=MESH
        )

    half[gx] = jnp.zeros((8, 128), F32)
    half[gx, 0:3, 0:S] = cen_ref[...]
    half[gx, 4:7, 0:S] = dis_ref[...]
    p8[...] = jnp.zeros((8, POINTS), F32)
    p8[0:3, :] = 16.0 * (pts_ref[...] - 0.5)
    sf[...] = jnp.zeros((16, NC), F32)
    for b in range(POINTS // 128):
        stack = left_stack(p8[:, b * 128 : (b + 1) * 128])
        left[b * 128 : (b + 1) * 128, :] = jnp.transpose(stack).astype(BF16)

    pl.semaphore_wait(barrier, N_GY - 1 + N_GX - 1)

    for k in range(1, N_GX):
        pltpu.make_async_remote_copy(
            src_ref=half.at[gx], dst_ref=half.at[gx], send_sem=ssem.at[0], recv_sem=rsem.at[0],
            device_id=(lax.rem(gx + k, N_GX), gy), device_id_type=MESH,
        ).start()
    seven = half.at[0 : N_GX - 1]
    pltpu.make_async_copy(seven, seven, rsem.at[0]).wait()
    lane = lax.broadcasted_iota(jnp.int32, (8, 128), 1)
    for zz in range(4):
        cbuf[zz, gy] = jnp.where(lane < S, half[2 * zz], pltpu.roll(half[2 * zz + 1], S, axis=1))
    for k in range(1, N_GY):
        pltpu.make_async_remote_copy(
            src_ref=cbuf.at[:, gy], dst_ref=cbuf.at[:, gy], send_sem=ssem.at[1], recv_sem=rsem.at[1],
            device_id=(gx, lax.rem(gy + k, N_GY)), device_id_type=MESH,
        ).start()

    own = cbuf[z, gy]
    own = jnp.where(rows8((8, 128)) < 3, 16.0 * (own - 0.5), 0.0)
    left[POINTS : POINTS + 128, :] = jnp.transpose(left_stack(own)).astype(BF16)
    fifteen = cbuf.at[:, 0 : N_GY - 1]
    pltpu.make_async_copy(fifteen, fifteen, rsem.at[1]).wait()

    def build(i, _):
        zz = lax.div(i, 2)
        g0 = lax.rem(i, 2) * 8
        cols = pl.ds(pl.multiple_of(i * 1024, 1024), 1024)
        t = jnp.concatenate([cbuf[zz, g0 + k] for k in range(8)], axis=1)
        x8 = jnp.where(rows8((8, 1024)) < 3, 16.0 * (t - 0.5), 0.0)
        right[:, cols] = right_stack(x8).astype(BF16)
        d_ref[:, cols] = jnp.concatenate([cbuf[zz, g0 + k, 4:8, :] for k in range(8)], axis=1)
        return 0

    lax.fori_loop(0, 8, build, 0)

    def fill_own(n, _):
        cols = pl.ds(pl.multiple_of(n * CHUNK, CHUNK), CHUNK)
        high, low = halves(bump(dot_nn(left[POINTS : POINTS + 128, :], right[:, cols])))
        kh[:, cols] = high
        kl[:, cols] = low
        return 0

    lax.fori_loop(0, NCHUNK, fill_own, 0)

    def fill_edges(n, _):
        cols = pl.ds(pl.multiple_of(n * CHUNK, CHUNK), CHUNK)
        for b in range(POINTS // 256):
            rows = slice(b * 256, (b + 1) * 256)
            high, low = halves(bump(dot_nn(left[rows, :], right[:, cols])))
            ph[rows, cols] = high
            plo[rows, cols] = low
        return 0

    def set_search(search):
        high = search.astype(BF16).astype(F32)
        sf[8:12, :] = high
        sf[12:16, :] = search - high

    def apply_own():
        sp[...] = sf[...].astype(BF16)
        product = dot_nt(kh[...], sp[...]) + dot_nt(kl[...], sp[...])
        t = jnp.transpose(product)
        return (t[8:12] + t[12:16]) * (1.0 / 256.0)

    def spread(buf, slot):
        for a, b, c in OFFSETS:
            zz = lax.rem(z + a, 4)
            to = (2 * zz + core, lax.rem(y + b, 4) * 4 + lax.rem(x + c, 4))
            pltpu.make_async_remote_copy(
                src_ref=buf.at[me], dst_ref=buf.at[me], send_sem=ssem.at[slot],
                recv_sem=rsem.at[slot], device_id=to, device_id_type=MESH,
            ).start()

    def arrive(buf, slot):
        rest = buf.at[0 : CHIPS - 1]
        pltpu.make_async_copy(rest, rest, rsem.at[slot]).wait()

    def collected(buf):
        return jnp.concatenate([buf[q] for q in range(CHIPS)], axis=1)

    def total(v):
        return jnp.sum(v, axis=1, keepdims=True)

    live = lax.broadcasted_iota(jnp.int32, (4, 1), 0) < 3

    def ratio(top, bottom):
        return top / jnp.where(live, bottom, 1.0)

    set_search(d_ref[...])
    g1[me] = apply_own()
    spread(g1, 2)
    lax.fori_loop(0, NCHUNK // 2, fill_edges, 0)
    arrive(g1, 2)
    d = d_ref[...]
    rr0 = total(d * d)
    applied = collected(g1) + SHIFT * d
    step = ratio(rr0, total(d * applied))
    remain = d - step * applied
    rr1 = total(remain * remain)
    search = remain + ratio(rr1, rr0) * d
    x_ref[...] = step * d
    r_ref[...] = remain
    s_ref[...] = search

    set_search(search)
    g2[me] = apply_own()
    spread(g2, 3)
    lax.fori_loop(NCHUNK // 2, NCHUNK, fill_edges, 0)
    arrive(g2, 3)
    search = s_ref[...]
    applied = collected(g2) + SHIFT * search
    step = ratio(rr1, total(search * applied))
    iterate = x_ref[...] + step * search
    remain = r_ref[...] - step * applied
    rr2 = total(remain * remain)
    search = remain + ratio(rr2, rr1) * search
    x_ref[...] = iterate
    s_ref[...] = search
    set_search(search)
    high = iterate.astype(BF16).astype(F32)
    sf[0:4, :] = high
    sf[4:8, :] = iterate - high

    mine = pl.ds(pl.multiple_of(me * 128, 128), 128)
    last = apply_own()
    own_search = s_ref[:, mine]
    g3[me] = own_search * (last + SHIFT * own_search)
    spread(g3, 4)

    lane4 = lax.broadcasted_iota(jnp.int32, (4, 128), 1) < S

    def evaluate(b, _):
        rows = pl.ds(pl.multiple_of(b * 128, 128), 128)
        t = jnp.transpose(dot_nt(ph[rows, :], sp[...]) + dot_nt(plo[rows, :], sp[...]))
        first = (t[0:4] + t[4:8]) * (1.0 / 256.0)
        second = (t[8:12] + t[12:16]) * (1.0 / 256.0)
        motion[2 * b] = jnp.where(lane4, first, pltpu.roll(second, S, axis=1))
        motion[2 * b + 1] = jnp.where(lane4, pltpu.roll(first, S, axis=1), second)
        return 0

    lax.fori_loop(0, POINTS // 128, evaluate, 0)

    for k in range(N_GY):
        to = lax.rem(gy + k, N_GY)
        for c in range(CAP):
            tile = motion[jnp.maximum(list_ref[to, c], 0)]
            if k == 0:
                inbox[gy, c] = tile
            else:
                outbox[k, c] = tile
    for k in range(1, N_GY):
        pltpu.make_async_remote_copy(
            src_ref=outbox.at[k], dst_ref=inbox.at[gy], send_sem=ssem.at[5], recv_sem=rsem.at[5],
            device_id=(gx, lax.rem(gy + k, N_GY)), device_id_type=MESH,
        ).start()

    arrive(g3, 4)
    summed = g3[0]
    for q in range(1, CHIPS):
        summed = summed + g3[q]
    step = ratio(rr2, total(summed))
    result = x_ref[:, mine] + step * s_ref[:, mine]
    result = jnp.where(core == 0, result, pltpu.roll(result, S, axis=1))
    coef_ref[...] = result[0:3, 0:S]

    box = inbox.at[0 : N_GY - 1]
    pltpu.make_async_copy(box, box, rsem.at[5]).wait()
    for s in range(N_GY):
        for c in range(CAP):
            tile = inbox[s, c]
            other = pltpu.roll(tile, S, axis=1)
            first = jnp.where(lane4, tile, other)
            second = jnp.where(lane4, other, tile)
            tile_ref[s * CAP + c] = first + step * second

    pltpu.make_async_copy(seven, seven, ssem.at[0]).wait()
    pltpu.make_async_copy(fifteen, fifteen, ssem.at[1]).wait()
    for buf, slot in ((g1, 2), (g2, 3), (g3, 4)):
        rest = buf.at[0 : CHIPS - 1]
        pltpu.make_async_copy(rest, rest, ssem.at[slot]).wait()
    pltpu.make_async_copy(box, box, ssem.at[5]).wait()


WIDTH = 512


def blend_kernel(table_ref, count_ref, tile_ref, out_ref, st, lhs):
    n = pl.program_id(0)

    @pl.when(n == 0)
    def _():
        for b in range(SLOTS):
            for e in range(12):
                st[e, 4 * b : 4 * b + 4, :] = tile_ref[table_ref[b, e]]
        lane = lax.broadcasted_iota(jnp.int32, (1, 128), 1)
        w1 = jnp.where(lane < S, lane, lane - S).astype(F32) / (S - 1)
        w0 = 1.0 - w1
        first = jnp.concatenate([st[e] for e in range(4)], axis=0)
        edge = first - 2.0 * (w0 * first[:, 0:1] + w1 * first[:, S - 1 : S])
        wide = jnp.concatenate(
            [edge, jnp.broadcast_to(w0, (16, 128)), jnp.broadcast_to(w1, (16, 128)),
             jnp.zeros((32, 128), F32)],
            axis=0,
        )
        base = jnp.transpose(wide)[0:S]
        high = base.astype(BF16).astype(F32)
        low = base - high
        col = lax.rem(lax.broadcasted_iota(jnp.int32, (S, 128), 1), 16)
        for b in range(SLOTS):
            alive = b < count_ref[0]
            for c in range(3):
                keep = jnp.logical_and(col == 4 * b + c, alive)
                kh = jnp.where(keep, high, 0.0).astype(BF16)
                rows = slice((b * 3 + c) * S, (b * 3 + c + 1) * S)
                lhs[rows, 0:128] = kh
                lhs[rows, 128:256] = kh
                lhs[rows, 256:384] = jnp.where(keep, low, 0.0).astype(BF16)

    spot = n * WIDTH + lax.broadcasted_iota(jnp.int32, (128, WIDTH), 1)
    pick = jnp.where(lax.shift_right_logical(spot, 6) == lax.broadcasted_iota(jnp.int32, (128, WIDTH), 0), 1.0, 0.0).astype(BF16)
    second = jnp.concatenate([st[e] for e in range(4, 8)], axis=0)
    h, m, l = parts(second)
    spread = dot_nn(jnp.concatenate([h, m, l], axis=0).astype(BF16), pick)
    spread = spread[0:64] + spread[64:128] + spread[128:192]
    flat = n * WIDTH + lax.broadcasted_iota(jnp.int32, (16, WIDTH), 1)
    j1 = lax.shift_right_logical(flat, 6).astype(F32) / (S - 1)
    k1 = jnp.bitwise_and(flat, 63).astype(F32) / (S - 1)
    j0 = 1.0 - j1
    k0 = 1.0 - k1
    third = [jnp.concatenate([st[e]] * (WIDTH // 128), axis=1) for e in range(8, 12)]
    h0 = spread[0:16] * k0 + spread[32:48] * k1 + third[0] * j0 + third[2] * j1
    h1 = spread[16:32] * k0 + spread[48:64] * k1 + third[1] * j0 + third[3] * j1
    rhs = jnp.concatenate(
        [j0 * k0, j1 * k0, j0 * k1, j1 * k1, h0, h1, jnp.zeros((32, WIDTH), F32)], axis=0
    )
    rh, rl = halves(rhs)
    full = dot_nn(lhs[...], jnp.concatenate([rh, rl, rh], axis=0))
    for b in range(SLOTS):
        for c in range(3):
            out_ref[b, c] = full[(b * 3 + c) * S : (b * 3 + c + 1) * S]


def shards(center_points, displacements, edge_points, send_list, block_tiles, block_count):
    vmem = pl.BlockSpec(memory_space=pltpu.VMEM)
    smem = pl.BlockSpec(memory_space=pltpu.SMEM)
    coefficients, tiles = pl.pallas_call(
        motion_kernel,
        out_shape=(
            jax.ShapeDtypeStruct((3, S), F32),
            jax.ShapeDtypeStruct((N_GY * CAP, 4, 128), F32),
        ),
        in_specs=[vmem, vmem, vmem, smem],
        out_specs=(vmem, vmem),
        scratch_shapes=[
            pltpu.VMEM((N_GX, 8, 128), F32),
            pltpu.VMEM((4, N_GY, 8, 128), F32),
            pltpu.VMEM((CHIPS, 4, 128), F32),
            pltpu.VMEM((CHIPS, 4, 128), F32),
            pltpu.VMEM((CHIPS, 4, 128), F32),
            pltpu.VMEM((64, NC), BF16),
            pltpu.VMEM((POINTS + 128, 64), BF16),
            pltpu.VMEM((128, NC), BF16),
            pltpu.VMEM((128, NC), BF16),
            pltpu.VMEM((POINTS, NC), BF16),
            pltpu.VMEM((POINTS, NC), BF16),
            pltpu.VMEM((16, NC), F32),
            pltpu.VMEM((16, NC), BF16),
            pltpu.VMEM((4, NC), F32),
            pltpu.VMEM((4, NC), F32),
            pltpu.VMEM((4, NC), F32),
            pltpu.VMEM((4, NC), F32),
            pltpu.VMEM((EDGE_DEV, 4, 128), F32),
            pltpu.VMEM((N_GY, CAP, 4, 128), F32),
            pltpu.VMEM((N_GY, CAP, 4, 128), F32),
            pltpu.VMEM((8, POINTS), F32),
            pltpu.SemaphoreType.DMA((6,)),
            pltpu.SemaphoreType.DMA((6,)),
        ],
        compiler_params=pltpu.CompilerParams(
            collective_id=0, has_side_effects=True, vmem_limit_bytes=60 * 1024 * 1024
        ),
        name="motion",
    )(center_points, displacements, edge_points, send_list[0])
    block_motion = pl.pallas_call(
        blend_kernel,
        grid=(S * S // WIDTH,),
        out_shape=jax.ShapeDtypeStruct((SLOTS, 3, S, S * S), F32),
        in_specs=[smem, smem, vmem],
        out_specs=pl.BlockSpec((SLOTS, 3, S, WIDTH), lambda n: (0, 0, 0, n)),
        scratch_shapes=[
            pltpu.VMEM((12, 16, 128), F32),
            pltpu.VMEM((SLOTS * 3 * S, 384), BF16),
        ],
        name="blend",
    )(block_tiles, block_count, tiles)
    return (coefficients, block_motion)


def solution(mesh):
    return jax.shard_map(
        shards,
        mesh=mesh,
        in_specs=(
            P(None, ("gx", "gy")),
            P(None, ("gx", "gy")),
            P(None, ("gx", "gy")),
            P(("gx", "gy"), None, None),
            P(("gx", "gy"), None),
            P(("gx", "gy")),
        ),
        out_specs=(P(None, ("gx", "gy")), P(("gx", "gy"), None, None, None)),
        check_vma=False,
    )
```

```python
import functools

import jax
import jax.numpy as jnp
from jax import lax
from jax.experimental import pallas as pl
from jax.experimental.pallas import tpu as pltpu
from jax.sharding import PartitionSpec as P

MESH = pl.DeviceIdType.MESH
F32 = jnp.float32
BF16 = jnp.bfloat16

NC = 8192
S = 64
SLOTS = 4
EDGE_DEV = 16
CAP = 3
N_GX = 8
N_GY = 16
CHIPS = 64
POINTS = EDGE_DEV * S
SHIFT = 0.1
CHUNK = 256
NCHUNK = NC // CHUNK
RING = (0, 1, 2, 1)
OFFSETS = sorted(
    [(a, b, c) for a in range(4) for b in range(4) for c in range(4) if (a, b, c) != (0, 0, 0)],
    key=lambda o: -sum(RING[q] for q in o),
)


def dot_nn(left, right):
    return lax.dot_general(left, right, (((1,), (0,)), ((), ())), preferred_element_type=F32)


def dot_nt(left, right):
    return lax.dot_general(left, right, (((1,), (1,)), ((), ())), preferred_element_type=F32)


def bump(squared):
    squared = jnp.maximum(squared, 1e-30)
    root = squared * lax.rsqrt(squared)
    t = jnp.maximum(4.0 - root, 0.0)
    t2 = t * t
    return (t2 * t2) * (5.0 - t)


def halves(v):
    high = v.astype(BF16)
    return high, (v - high.astype(F32)).astype(BF16)


def parts(v):
    high = v.astype(BF16).astype(F32)
    rest = v - high
    mid = rest.astype(BF16).astype(F32)
    return high, mid, rest - mid


def rows8(shape):
    return lax.broadcasted_iota(jnp.int32, shape, 0)


def left_stack(x8):
    row = rows8(x8.shape)
    norm = jnp.sum(x8 * x8, axis=0, keepdims=True)
    v = jnp.where(row < 3, -2.0 * x8, jnp.where(row == 3, 1.0, jnp.where(row == 4, norm, 0.0)))
    h, m, l = parts(v)
    return jnp.concatenate([h, h, m, m, h, l, jnp.zeros_like(h), jnp.zeros_like(h)], axis=0)


def right_stack(x8):
    row = rows8(x8.shape)
    norm = jnp.sum(x8 * x8, axis=0, keepdims=True)
    v = jnp.where(row < 3, x8, jnp.where(row == 3, norm, jnp.where(row == 4, 1.0, 0.0)))
    h, m, l = parts(v)
    return jnp.concatenate([h, m, h, m, l, h, jnp.zeros_like(h), jnp.zeros_like(h)], axis=0)


STORED = 20
EARLY = 2
FIRST = 9
PER = 3
TALL = 64
AHEAD = 2


def motion_kernel(
    cen_ref, dis_ref, pts_ref, list_ref, coef_ref, tile_ref,
    half, cpos, cdis, g1, g2, g3, cst, pst, ost, own_k, stored, fresh, acc, sf, sp, xs,
    d_ref, x_ref, r_ref, s_ref, motion, outbox, inbox, p8, ssem, rsem,
):
    gx = lax.axis_index("gx")
    gy = lax.axis_index("gy")
    z = lax.div(gx, 2)
    core = lax.rem(gx, 2)
    y = lax.div(gy, 4)
    x = lax.rem(gy, 4)
    me = gy * 4 + z

    barrier = pltpu.get_barrier_semaphore()
    for k in range(1, N_GY):
        pl.semaphore_signal(
            barrier, inc=1, device_id=(gx, lax.rem(gy + k, N_GY)), device_id_type=MESH
        )
    for k in range(1, N_GX):
        pl.semaphore_signal(
            barrier, inc=1, device_id=(lax.rem(gx + k, N_GX), gy), device_id_type=MESH
        )

    half[gx] = jnp.zeros((8, 128), F32)
    half[gx, 0:3, 0:S] = cen_ref[...]
    half[gx, 4:7, 0:S] = dis_ref[...]
    p8[...] = jnp.zeros((8, POINTS), F32)
    p8[0:3, :] = 16.0 * (pts_ref[...] - 0.5)
    sf[...] = jnp.zeros((16, NC), F32)
    xs[...] = jnp.zeros((8, 512), F32)
    for b in range(POINTS // 128):
        cols = slice(b * 128, (b + 1) * 128)
        pst[:, cols] = left_stack(p8[:, cols]).astype(BF16)
    acc[...] = jnp.zeros((16, POINTS), F32)
    fresh[...] = jnp.zeros((8, 4 * CHUNK, 128), BF16)

    pl.semaphore_wait(barrier, N_GY - 1 + N_GX - 1)

    for k in range(1, N_GX):
        pltpu.make_async_remote_copy(
            src_ref=half.at[gx], dst_ref=half.at[gx], send_sem=ssem.at[0], recv_sem=rsem.at[0],
            device_id=(lax.rem(gx + k, N_GX), gy), device_id_type=MESH,
        ).start()
    seven = half.at[0 : N_GX - 1]
    pltpu.make_async_copy(seven, seven, rsem.at[0]).wait()
    lane = lax.broadcasted_iota(jnp.int32, (8, 128), 1)
    for zz in range(4):
        both = jnp.where(lane < S, half[2 * zz], pltpu.roll(half[2 * zz + 1], S, axis=1))
        cpos[gy, zz] = both[0:4]
        cdis[gy, zz] = both[4:8]
    for buf, slot in ((cpos, 1), (cdis, 6)):
        for k in range(1, N_GY):
            pltpu.make_async_remote_copy(
                src_ref=buf.at[gy], dst_ref=buf.at[gy], send_sem=ssem.at[slot],
                recv_sem=rsem.at[slot], device_id=(gx, lax.rem(gy + k, N_GY)),
                device_id_type=MESH,
            ).start()

    def centred(t):
        return jnp.where(rows8(t.shape) < 3, 16.0 * (t - 0.5), 0.0)

    def build(k, _):
        line = lax.rem(gy + k, N_GY)
        rows = pl.ds(pl.multiple_of(k * 512, 512), 512)
        xs[0:4, :] = centred(jnp.concatenate([cpos[line, zz] for zz in range(4)], axis=1))
        cst[rows, :] = jnp.transpose(right_stack(xs[...])).astype(BF16)
        return 0

    def fill_own(n, _):
        rows = pl.ds(pl.multiple_of(n * CHUNK, CHUNK), CHUNK)
        base = pl.multiple_of(n * (2 * CHUNK), 2 * CHUNK)
        high, low = halves(bump(dot_nn(cst[rows, :], ost[...])))
        own_k[pl.ds(base, CHUNK), :] = high
        own_k[pl.ds(base + CHUNK, CHUNK), :] = low
        return 0

    def fill(dst, jobs, extras):
        blocks = [
            (n, base, jb, pp)
            for n, base in jobs
            for jb in range(CHUNK // TALL)
            for pp in range(POINTS // 256)
        ]

        def distance(block):
            n, _, jb, pp = block
            rows = pl.ds(pl.multiple_of(n * CHUNK + jb * TALL, TALL), TALL)
            return dot_nn(cst[rows, :], pst[:, pp * 256 : (pp + 1) * 256])

        ready = [distance(block) for block in blocks[:AHEAD]]
        for at, (n, base, jb, pp) in enumerate(blocks):
            if at + AHEAD < len(blocks):
                ready.append(distance(blocks[at + AHEAD]))
            for extra in extras.get(at, ()):
                extra()
            high, low = halves(bump(ready.pop(0)))
            for half_at in range(2):
                part = slice(half_at * 128, half_at * 128 + 128)
                dst[2 * pp + half_at, pl.ds(base + jb * TALL, TALL), :] = high[:, part]
                dst[2 * pp + half_at, pl.ds(base + CHUNK + jb * TALL, TALL), :] = low[:, part]

    def fill_edges(n, _):
        fill(stored, [(n, pl.multiple_of(n * (2 * CHUNK), 2 * CHUNK))], {})
        return 0

    build(0, 0)
    p8[:, 0:128] = jnp.zeros((8, 128), F32)
    p8[0:4, 0:128] = centred(cpos[gy, z])
    ost[...] = left_stack(p8[:, 0:128]).astype(BF16)
    lax.fori_loop(0, EARLY, fill_own, 0)
    lax.fori_loop(0, EARLY, fill_edges, 0)

    fifteen = cpos.at[0 : N_GY - 1]
    pltpu.make_async_copy(fifteen, fifteen, rsem.at[1]).wait()
    lax.fori_loop(1, N_GY, build, 0)
    lax.fori_loop(EARLY, NCHUNK, fill_own, 0, unroll=2)
    others = cdis.at[0 : N_GY - 1]
    pltpu.make_async_copy(others, others, rsem.at[6]).wait()
    order = [(lax.rem(gy + k, N_GY), zz) for k in range(N_GY) for zz in range(4)]
    d_ref[...] = jnp.concatenate([cdis[line, zz] for line, zz in order], axis=1)

    def set_search(search):
        high = search.astype(BF16).astype(F32)
        sf[8:12, :] = high
        sf[12:16, :] = search - high

    def apply_own():
        for n in range(NCHUNK):
            value = sf[:, n * CHUNK : (n + 1) * CHUNK].astype(BF16)
            sp[:, 2 * n * CHUNK : (2 * n + 1) * CHUNK] = value
            sp[:, (2 * n + 1) * CHUNK : (2 * n + 2) * CHUNK] = value
        t = dot_nn(sp[...], own_k[...])
        return (t[8:12] + t[12:16]) * (1.0 / 256.0)

    def spread(buf, slot):
        for a, b, c in OFFSETS:
            zz = lax.rem(z + a, 4)
            to = (2 * zz + core, lax.rem(y + b, 4) * 4 + lax.rem(x + c, 4))
            pltpu.make_async_remote_copy(
                src_ref=buf.at[me], dst_ref=buf.at[me], send_sem=ssem.at[slot],
                recv_sem=rsem.at[slot], device_id=to, device_id_type=MESH,
            ).start()

    def arrive(buf, slot):
        rest = buf.at[0 : CHIPS - 1]
        pltpu.make_async_copy(rest, rest, rsem.at[slot]).wait()

    def collected(buf):
        return jnp.concatenate([buf[line * 4 + zz] for line, zz in order], axis=1)

    def total(v):
        return jnp.sum(v, axis=1, keepdims=True)

    live = lax.broadcasted_iota(jnp.int32, (4, 1), 0) < 3

    def ratio(top, bottom):
        return top / jnp.where(live, bottom, 1.0)

    set_search(d_ref[...])
    g1[me] = apply_own()
    spread(g1, 2)
    lax.fori_loop(EARLY, EARLY + FIRST, fill_edges, 0)
    arrive(g1, 2)
    d = d_ref[...]
    rr0 = total(d * d)
    applied = collected(g1) + SHIFT * d
    step = ratio(rr0, total(d * applied))
    remain = d - step * applied
    rr1 = total(remain * remain)
    search = remain + ratio(rr1, rr0) * d
    x_ref[...] = step * d
    r_ref[...] = remain
    s_ref[...] = search

    set_search(search)
    g2[me] = apply_own()
    spread(g2, 3)
    lax.fori_loop(EARLY + FIRST, STORED, fill_edges, 0)
    arrive(g2, 3)
    search = s_ref[...]
    applied = collected(g2) + SHIFT * search
    step = ratio(rr1, total(search * applied))
    iterate = x_ref[...] + step * search
    remain = r_ref[...] - step * applied
    rr2 = total(remain * remain)
    search = remain + ratio(rr2, rr1) * search
    x_ref[...] = iterate
    s_ref[...] = search
    set_search(search)
    high = iterate.astype(BF16).astype(F32)
    sf[0:4, :] = high
    sf[4:8, :] = iterate - high

    mine = pl.ds(pl.multiple_of(z * 128, 128), 128)
    last = apply_own()
    own_search = s_ref[:, mine]
    g3[me] = own_search * (last + SHIFT * own_search)
    spread(g3, 4)

    lane4 = lax.broadcasted_iota(jnp.int32, (4, 128), 1) < S

    def contract(src, n, base, pp):
        lhs = sp[:, pl.ds(pl.multiple_of(n * (2 * CHUNK), 2 * CHUNK), 2 * CHUNK)]
        rows = pl.ds(base, 2 * CHUNK)
        cols = slice(pp * 256, (pp + 1) * 256)
        rhs = jnp.concatenate([src[2 * pp, rows, :], src[2 * pp + 1, rows, :]], axis=1)
        acc[:, cols] += dot_nn(lhs, rhs)

    def held(n, pp):
        contract(stored, n, pl.multiple_of(n * (2 * CHUNK), 2 * CHUNK), pp)

    def fused(i, _):
        now = STORED + 2 * i
        across = POINTS // 256
        blocks = 2 * (CHUNK // TALL) * across
        extras = {}
        for c in range(2):
            for pp in range(across):
                at = c * (blocks // 2) + pp
                extras.setdefault(at, []).append(
                    functools.partial(contract, fresh, now - 2 + c, c * 2 * CHUNK, pp)
                )
        places = [at for at in range(blocks) if at % (blocks // 2) >= across]
        pieces = [(n, pp) for n in range(PER) for pp in range(across)]
        for k, (n, pp) in enumerate(pieces):
            at = places[k * len(places) // len(pieces)]
            extras.setdefault(at, []).append(functools.partial(held, PER * i + n, pp))
        fill(fresh, [(now, 0), (now + 1, 2 * CHUNK)], extras)
        return 0

    turns = (NCHUNK - STORED) // 2
    lax.fori_loop(0, turns, fused, 0)
    for pp in range(POINTS // 256):
        for c in range(2):
            contract(fresh, NCHUNK - 2 + c, c * 2 * CHUNK, pp)
        for n in range(PER * turns, STORED):
            held(n, pp)

    for b in range(POINTS // 128):
        t = acc[:, b * 128 : (b + 1) * 128]
        first = (t[0:4] + t[4:8]) * (1.0 / 256.0)
        second = (t[8:12] + t[12:16]) * (1.0 / 256.0)
        motion[2 * b] = jnp.where(lane4, first, pltpu.roll(second, S, axis=1))
        motion[2 * b + 1] = jnp.where(lane4, pltpu.roll(first, S, axis=1), second)

    for k in range(N_GY):
        to = lax.rem(gy + k, N_GY)
        for c in range(CAP):
            tile = motion[jnp.maximum(list_ref[c, 0, to], 0)]
            if k == 0:
                inbox[gy, c] = tile
            else:
                outbox[k, c] = tile
    for k in range(1, N_GY):
        pltpu.make_async_remote_copy(
            src_ref=outbox.at[k], dst_ref=inbox.at[gy], send_sem=ssem.at[5], recv_sem=rsem.at[5],
            device_id=(gx, lax.rem(gy + k, N_GY)), device_id_type=MESH,
        ).start()

    arrive(g3, 4)
    summed = g3[0]
    for q in range(1, CHIPS):
        summed = summed + g3[q]
    step = ratio(rr2, total(summed))
    result = x_ref[:, mine] + step * s_ref[:, mine]
    result = jnp.where(core == 0, result, pltpu.roll(result, S, axis=1))
    coef_ref[...] = result[0:3, 0:S]

    pltpu.make_async_copy(seven, seven, ssem.at[0]).wait()
    pltpu.make_async_copy(fifteen, fifteen, ssem.at[1]).wait()
    pltpu.make_async_copy(others, others, ssem.at[6]).wait()
    for buf, slot in ((g1, 2), (g2, 3), (g3, 4)):
        rest = buf.at[0 : CHIPS - 1]
        pltpu.make_async_copy(rest, rest, ssem.at[slot]).wait()

    box = inbox.at[0 : N_GY - 1]
    pltpu.make_async_copy(box, box, rsem.at[5]).wait()
    for s in range(N_GY):
        for c in range(CAP):
            tile = inbox[s, c]
            other = pltpu.roll(tile, S, axis=1)
            first = jnp.where(lane4, tile, other)
            second = jnp.where(lane4, other, tile)
            tile_ref[s * CAP + c] = first + step * second
    pltpu.make_async_copy(box, box, ssem.at[5]).wait()


WIDTH = 512


def blend_kernel(table_ref, count_ref, tile_ref, coef_ref, out_ref, copy_ref, st, lhs):
    n = pl.program_id(0)

    @pl.when(n == 0)
    def _():
        copy_ref[...] = coef_ref[...]
        for b in range(SLOTS):
            for e in range(12):
                row = e * 12 + 3 * b
                st[row : row + 3, :] = tile_ref[table_ref[b, e]][0:3]
        lane = lax.broadcasted_iota(jnp.int32, (1, 128), 1)
        w1 = jnp.where(lane < S, lane, lane - S).astype(F32) / (S - 1)
        w0 = 1.0 - w1
        first = st[0:48, :]
        edge = first - 2.0 * (w0 * first[:, 0:1] + w1 * first[:, S - 1 : S])
        ramps = jnp.where(rows8((24, 128)) < 12, w0, w1)
        wide = jnp.concatenate([edge, ramps, jnp.zeros((8, 128), F32)], axis=0)
        high = wide.astype(BF16).astype(F32)
        stack = jnp.concatenate([high, high, wide - high, jnp.zeros((16, 128), F32)], axis=0)
        base = jnp.transpose(stack)[0:S]
        col = lax.rem(lax.rem(lax.broadcasted_iota(jnp.int32, (S, 256), 1), 80), 12)
        for b in range(SLOTS):
            alive = b < count_ref[0]
            for c in range(3):
                slot = 3 * b + c
                keep = jnp.logical_and(col == slot, alive)
                lhs[slot * S : (slot + 1) * S, :] = jnp.where(keep, base, 0.0).astype(BF16)

    spot = n * WIDTH + lax.broadcasted_iota(jnp.int32, (128, WIDTH), 1)
    cell = lax.broadcasted_iota(jnp.int32, (128, WIDTH), 0)
    pick = jnp.where(lax.shift_right_logical(spot, 6) == cell, 1.0, 0.0).astype(BF16)
    h, m, l = parts(st[48:96, :])
    spread = dot_nn(jnp.concatenate([h, m, l], axis=0).astype(BF16), pick)
    spread = spread[0:48] + spread[48:96] + spread[96:144]
    flat = n * WIDTH + lax.broadcasted_iota(jnp.int32, (8, WIDTH), 1)[0:1]
    j1 = lax.shift_right_logical(flat, 6).astype(F32) / (S - 1)
    k1 = jnp.bitwise_and(flat, 63).astype(F32) / (S - 1)
    j0 = 1.0 - j1
    k0 = 1.0 - k1
    third = jnp.concatenate([st[96:144, :]] * (WIDTH // 128), axis=1)
    sides = spread[0:24] * k0 + spread[24:48] * k1 + third[0:24] * j0 + third[24:48] * j1
    group = rows8((48, WIDTH))
    odd = jnp.logical_or(
        jnp.logical_and(group >= 12, group < 24), group >= 36
    )
    corner = jnp.where(odd, j1, j0) * jnp.where(group < 24, k0, k1)
    rh, rl = halves(jnp.concatenate([corner, sides, jnp.zeros((8, WIDTH), F32)], axis=0))
    rhs = jnp.concatenate([rh, rl, rh, jnp.zeros((16, WIDTH), BF16)], axis=0)
    full = dot_nn(lhs[...], rhs)
    for b in range(SLOTS):
        for c in range(3):
            out_ref[b, c] = full[(b * 3 + c) * S : (b * 3 + c + 1) * S]


def shards(center_points, displacements, edge_points, send_list, block_tiles, block_count):
    vmem = pl.BlockSpec(memory_space=pltpu.VMEM)
    smem = pl.BlockSpec(memory_space=pltpu.SMEM)
    coefficients, tiles = pl.pallas_call(
        motion_kernel,
        out_shape=(
            jax.ShapeDtypeStruct((3, S), F32),
            jax.ShapeDtypeStruct((N_GY * CAP, 4, 128), F32),
        ),
        in_specs=[vmem, vmem, vmem, smem],
        out_specs=(vmem, vmem),
        scratch_shapes=[
            pltpu.VMEM((N_GX, 8, 128), F32),
            pltpu.VMEM((N_GY, 4, 4, 128), F32),
            pltpu.VMEM((N_GY, 4, 4, 128), F32),
            pltpu.VMEM((CHIPS, 4, 128), F32),
            pltpu.VMEM((CHIPS, 4, 128), F32),
            pltpu.VMEM((CHIPS, 4, 128), F32),
            pltpu.VMEM((NC, 64), BF16),
            pltpu.VMEM((64, POINTS), BF16),
            pltpu.VMEM((64, 128), BF16),
            pltpu.VMEM((2 * NC, 128), BF16),
            pltpu.VMEM((POINTS // 128, STORED * 2 * CHUNK, 128), BF16),
            pltpu.VMEM((POINTS // 128, 4 * CHUNK, 128), BF16),
            pltpu.VMEM((16, POINTS), F32),
            pltpu.VMEM((16, NC), F32),
            pltpu.VMEM((16, 2 * NC), BF16),
            pltpu.VMEM((8, 512), F32),
            pltpu.VMEM((4, NC), F32),
            pltpu.VMEM((4, NC), F32),
            pltpu.VMEM((4, NC), F32),
            pltpu.VMEM((4, NC), F32),
            pltpu.VMEM((EDGE_DEV, 4, 128), F32),
            pltpu.VMEM((N_GY, CAP, 4, 128), F32),
            pltpu.VMEM((N_GY, CAP, 4, 128), F32),
            pltpu.VMEM((8, POINTS), F32),
            pltpu.SemaphoreType.DMA((7,)),
            pltpu.SemaphoreType.DMA((7,)),
        ],
        compiler_params=pltpu.CompilerParams(
            collective_id=0, has_side_effects=True, vmem_limit_bytes=60 * 1024 * 1024
        ),
        name="motion",
    )(center_points, displacements, edge_points, send_list.transpose(2, 0, 1))
    block_motion, coefficients = pl.pallas_call(
        blend_kernel,
        grid=(S * S // WIDTH,),
        out_shape=(
            jax.ShapeDtypeStruct((SLOTS, 3, S, S * S), F32),
            jax.ShapeDtypeStruct((3, S), F32),
        ),
        in_specs=[smem, smem, vmem, pl.BlockSpec((3, S), lambda n: (0, 0))],
        out_specs=(
            pl.BlockSpec((SLOTS, 3, S, WIDTH), lambda n: (0, 0, 0, n)),
            pl.BlockSpec((3, S), lambda n: (0, 0)),
        ),
        scratch_shapes=[
            pltpu.VMEM((144, 128), F32),
            pltpu.VMEM((SLOTS * 3 * S, 256), BF16),
        ],
        name="blend",
    )(block_tiles, block_count, tiles, coefficients)
    return (coefficients, block_motion)


def solution(mesh):
    return jax.shard_map(
        shards,
        mesh=mesh,
        in_specs=(
            P(None, ("gx", "gy")),
            P(None, ("gx", "gy")),
            P(None, ("gx", "gy")),
            P(("gx", "gy"), None, None),
            P(("gx", "gy"), None),
            P(("gx", "gy")),
        ),
        out_specs=(P(None, ("gx", "gy")), P(("gx", "gy"), None, None, None)),
        check_vma=False,
    )
```

```python
import functools

import jax
import jax.numpy as jnp
from jax import lax
from jax.experimental import pallas as pl
from jax.experimental.pallas import tpu as pltpu
from jax.sharding import PartitionSpec as P

MESH = pl.DeviceIdType.MESH
F32 = jnp.float32
BF16 = jnp.bfloat16

NC = 8192
S = 64
SLOTS = 4
EDGE_DEV = 16
CAP = 3
N_GX = 8
N_GY = 16
CHIPS = 64
POINTS = EDGE_DEV * S
SHIFT = 0.1
CHUNK = 256
NCHUNK = NC // CHUNK
RING = (0, 1, 2, 1)


def dot_nn(left, right):
    return lax.dot_general(left, right, (((1,), (0,)), ((), ())), preferred_element_type=F32)


def dot_nt(left, right):
    return lax.dot_general(left, right, (((1,), (1,)), ((), ())), preferred_element_type=F32)


def bump(squared):
    squared = jnp.maximum(squared, 1e-30)
    root = squared * lax.rsqrt(squared)
    t = jnp.maximum(4.0 - root, 0.0)
    t2 = t * t
    return (t2 * t2) * (5.0 - t)


def halves(v):
    high = v.astype(BF16)
    return high, (v - high.astype(F32)).astype(BF16)


def parts(v):
    high = v.astype(BF16).astype(F32)
    rest = v - high
    mid = rest.astype(BF16).astype(F32)
    return high, mid, rest - mid


def rows8(shape):
    return lax.broadcasted_iota(jnp.int32, shape, 0)


def left_stack(x8):
    row = rows8(x8.shape)
    norm = jnp.sum(x8 * x8, axis=0, keepdims=True)
    v = jnp.where(row < 3, -2.0 * x8, jnp.where(row == 3, 1.0, jnp.where(row == 4, norm, 0.0)))
    h, m, l = parts(v)
    return jnp.concatenate([h, h, m, m, h, l, jnp.zeros_like(h), jnp.zeros_like(h)], axis=0)


def right_stack(x8):
    row = rows8(x8.shape)
    norm = jnp.sum(x8 * x8, axis=0, keepdims=True)
    v = jnp.where(row < 3, x8, jnp.where(row == 3, norm, jnp.where(row == 4, 1.0, 0.0)))
    h, m, l = parts(v)
    return jnp.concatenate([h, m, h, m, l, h, jnp.zeros_like(h), jnp.zeros_like(h)], axis=0)


EARLY = 6
FIRST = 10
GROUP = 2
STORED = EARLY + 2 * FIRST
TALL = 64
AHEAD = 2
OFFSETS = sorted(
    [(a, b, c) for a in range(4) for b in range(4) for c in range(4) if (a, b, c) != (0, 0, 0)],
    key=lambda o: -sum(RING[q] for q in o),
)
LINES = sorted(((a, b) for a in range(4) for b in range(4)), key=lambda o: RING[o[0]] + RING[o[1]])
NEAR = 5


def motion_kernel(
    cen_ref, dis_ref, pts_ref, list_ref, coef_ref, tile_ref,
    half, cpos, cdis, g1, g2, g3, cst, pst, ost, own_k, stored, fresh, acc, sf, sp, xs,
    d_ref, x_ref, r_ref, s_ref, motion, outbox, inbox, p8, ssem, rsem,
):
    gx = lax.axis_index("gx")
    gy = lax.axis_index("gy")
    z = lax.div(gx, 2)
    core = lax.rem(gx, 2)
    y = lax.div(gy, 4)
    x = lax.rem(gy, 4)
    me = gy * 4 + z
    lines = [lax.rem(y + a, 4) * 4 + lax.rem(x + b, 4) for a, b in LINES]

    barrier = pltpu.get_barrier_semaphore()
    for k in range(1, N_GY):
        pl.semaphore_signal(
            barrier, inc=1, device_id=(gx, lines[k]), device_id_type=MESH
        )
    for k in range(1, N_GX):
        pl.semaphore_signal(
            barrier, inc=1, device_id=(lax.rem(gx + k, N_GX), gy), device_id_type=MESH
        )

    half[gx] = jnp.zeros((8, 128), F32)
    half[gx, 0:3, 0:S] = cen_ref[...]
    half[gx, 4:7, 0:S] = dis_ref[...]
    p8[...] = jnp.zeros((8, POINTS), F32)
    p8[0:3, :] = 16.0 * (pts_ref[...] - 0.5)
    sf[...] = jnp.zeros((16, NC), F32)
    xs[...] = jnp.zeros((4, 8, 512), F32)
    for b in range(POINTS // 128):
        cols = slice(b * 128, (b + 1) * 128)
        pst[:, cols] = left_stack(p8[:, cols]).astype(BF16)
    acc[...] = jnp.zeros((16, POINTS), F32)
    fresh[...] = jnp.zeros((8, 4 * CHUNK, 128), BF16)

    pl.semaphore_wait(barrier, N_GY - 1 + N_GX - 1)

    for k in range(1, N_GX):
        pltpu.make_async_remote_copy(
            src_ref=half.at[gx], dst_ref=half.at[gx], send_sem=ssem.at[0], recv_sem=rsem.at[0],
            device_id=(lax.rem(gx + k, N_GX), gy), device_id_type=MESH,
        ).start()
    seven = half.at[0 : N_GX - 1]
    pltpu.make_async_copy(seven, seven, rsem.at[0]).wait()
    lane = lax.broadcasted_iota(jnp.int32, (8, 128), 1)
    for zz in range(4):
        both = jnp.where(lane < S, half[2 * zz], pltpu.roll(half[2 * zz + 1], S, axis=1))
        cpos[gy, zz] = both[0:4]
        cdis[gy, zz] = both[4:8]
    def to_plane(src, dst, slot, far):
        for k in range(1, N_GY):
            pltpu.make_async_remote_copy(
                src_ref=src, dst_ref=dst, send_sem=ssem.at[slot],
                recv_sem=rsem.at[slot if k < NEAR else far], device_id=(gx, lines[k]),
                device_id_type=MESH,
            ).start()

    to_plane(cpos.at[gy], cpos.at[gy], 1, 7)
    to_plane(cdis.at[gy], cdis.at[gy], 6, 6)

    def centred(t):
        return jnp.where(rows8(t.shape) < 3, 16.0 * (t - 0.5), 0.0)

    def build(k):
        line = lines[k]
        rows = slice(k * 512, k * 512 + 512)
        xs[k % 4, 0:4, :] = centred(jnp.concatenate([cpos[line, zz] for zz in range(4)], axis=1))
        cst[rows, :] = jnp.transpose(right_stack(xs[k % 4])).astype(BF16)

    def fill_own(n, _):
        rows = pl.ds(pl.multiple_of(n * CHUNK, CHUNK), CHUNK)
        base = pl.multiple_of(n * (2 * CHUNK), 2 * CHUNK)
        high, low = halves(bump(dot_nn(cst[rows, :], ost[...])))
        own_k[pl.ds(base, CHUNK), :] = high
        own_k[pl.ds(base + CHUNK, CHUNK), :] = low
        return 0

    def fill(dst, jobs, extras):
        blocks = [
            (n, base, jb, pp)
            for n, base in jobs
            for jb in range(CHUNK // TALL)
            for pp in range(POINTS // 256)
        ]

        def distance(block):
            n, _, jb, pp = block
            start = n * CHUNK + jb * TALL
            rows = pl.ds(start if isinstance(n, int) else pl.multiple_of(start, TALL), TALL)
            return dot_nn(cst[rows, :], pst[:, pp * 256 : (pp + 1) * 256])

        ready = [distance(block) for block in blocks[:AHEAD]]
        for at, (n, base, jb, pp) in enumerate(blocks):
            if at + AHEAD < len(blocks):
                ready.append(distance(blocks[at + AHEAD]))
            for extra in extras.get(at, ()):
                extra()
            high, low = halves(bump(ready.pop(0)))
            for half_at in range(2):
                part = slice(half_at * 128, half_at * 128 + 128)
                dst[2 * pp + half_at, pl.ds(base + jb * TALL, TALL), :] = high[:, part]
                dst[2 * pp + half_at, pl.ds(base + CHUNK + jb * TALL, TALL), :] = low[:, part]

    def fill_stored(first, count):
        def turn(i, _):
            n = first + i * GROUP
            fill(stored, [(n + k, row_of(n + k)) for k in range(GROUP)], {})
            return 0

        def row_of(n):
            return pl.multiple_of(n * (2 * CHUNK), 2 * CHUNK)

        whole = count // GROUP
        if whole:
            lax.fori_loop(0, whole, turn, 0)
        for n in range(first + whole * GROUP, first + count):
            fill(stored, [(n, n * 2 * CHUNK)], {})

    build(0)
    p8[:, 0:128] = jnp.zeros((8, 128), F32)
    p8[0:4, 0:128] = centred(cpos[gy, z])
    ost[...] = left_stack(p8[:, 0:128]).astype(BF16)
    lax.fori_loop(0, 2, fill_own, 0)
    fill_stored(0, 2)

    near = cpos.at[0 : NEAR - 1]
    pltpu.make_async_copy(near, near, rsem.at[1]).wait()
    for k in range(1, NEAR):
        build(k)
    lax.fori_loop(2, 2 * NEAR, fill_own, 0, unroll=4)
    fill_stored(2, EARLY - 2)

    far = cpos.at[0 : N_GY - NEAR]
    pltpu.make_async_copy(far, far, rsem.at[7]).wait()
    for k in range(NEAR, N_GY):
        build(k)
    lax.fori_loop(2 * NEAR, NCHUNK, fill_own, 0, unroll=2)
    fifteen = cpos.at[0 : N_GY - 1]
    others = cdis.at[0 : N_GY - 1]
    pltpu.make_async_copy(others, others, rsem.at[6]).wait()
    order = [(line, zz) for line in lines for zz in range(4)]
    d_ref[...] = jnp.concatenate([cdis[line, zz] for line, zz in order], axis=1)

    def set_search(search):
        high = search.astype(BF16).astype(F32)
        sf[8:12, :] = high
        sf[12:16, :] = search - high

    def apply_own():
        for n in range(NCHUNK):
            value = sf[:, n * CHUNK : (n + 1) * CHUNK].astype(BF16)
            sp[:, 2 * n * CHUNK : (2 * n + 1) * CHUNK] = value
            sp[:, (2 * n + 1) * CHUNK : (2 * n + 2) * CHUNK] = value
        t = dot_nn(sp[...], own_k[...])
        return (t[8:12] + t[12:16]) * (1.0 / 256.0)

    def spread(buf, slot):
        for a, b, c in OFFSETS:
            zz = lax.rem(z + a, 4)
            to = (2 * zz + core, lax.rem(y + b, 4) * 4 + lax.rem(x + c, 4))
            pltpu.make_async_remote_copy(
                src_ref=buf.at[me], dst_ref=buf.at[me], send_sem=ssem.at[slot],
                recv_sem=rsem.at[slot], device_id=to, device_id_type=MESH,
            ).start()

    def arrive(buf, slot):
        rest = buf.at[0 : CHIPS - 1]
        pltpu.make_async_copy(rest, rest, rsem.at[slot]).wait()

    def collected(buf):
        return jnp.concatenate([buf[line * 4 + zz] for line, zz in order], axis=1)

    def total(v):
        return jnp.sum(v, axis=1, keepdims=True)

    live = lax.broadcasted_iota(jnp.int32, (4, 1), 0) < 3

    def ratio(top, bottom):
        return top / jnp.where(live, bottom, 1.0)

    set_search(d_ref[...])
    g1[me] = apply_own()
    spread(g1, 2)
    fill_stored(EARLY, FIRST)
    arrive(g1, 2)
    d = d_ref[...]
    rr0 = total(d * d)
    applied = collected(g1) + SHIFT * d
    step = ratio(rr0, total(d * applied))
    remain = d - step * applied
    rr1 = total(remain * remain)
    search = remain + ratio(rr1, rr0) * d
    x_ref[...] = step * d
    r_ref[...] = remain
    s_ref[...] = search

    set_search(search)
    g2[me] = apply_own()
    spread(g2, 3)
    fill_stored(EARLY + FIRST, FIRST)
    arrive(g2, 3)
    search = s_ref[...]
    applied = collected(g2) + SHIFT * search
    step = ratio(rr1, total(search * applied))
    iterate = x_ref[...] + step * search
    remain = r_ref[...] - step * applied
    rr2 = total(remain * remain)
    search = remain + ratio(rr2, rr1) * search
    x_ref[...] = iterate
    s_ref[...] = search
    set_search(search)
    high = iterate.astype(BF16).astype(F32)
    sf[0:4, :] = high
    sf[4:8, :] = iterate - high

    mine = pl.ds(pl.multiple_of(z * 128, 128), 128)
    last = apply_own()
    own_search = s_ref[:, mine]
    g3[me] = own_search * (last + SHIFT * own_search)
    spread(g3, 4)

    lane4 = lax.broadcasted_iota(jnp.int32, (4, 128), 1) < S

    def at_chunk(n):
        return n * 2 * CHUNK if isinstance(n, int) else pl.multiple_of(n * (2 * CHUNK), 2 * CHUNK)

    def contract(src, n, base, pp):
        lhs = sp[:, pl.ds(at_chunk(n), 2 * CHUNK)]
        rows = pl.ds(base, 2 * CHUNK)
        cols = slice(pp * 256, (pp + 1) * 256)
        rhs = jnp.concatenate([src[2 * pp, rows, :], src[2 * pp + 1, rows, :]], axis=1)
        acc[:, cols] += dot_nn(lhs, rhs)

    def held(n, pp):
        contract(stored, n, at_chunk(n), pp)

    turns = (NCHUNK - STORED) // 2
    per = STORED // turns

    def fused(i, _):
        now = STORED + 2 * i
        across = POINTS // 256
        blocks = 2 * (CHUNK // TALL) * across
        extras = {}
        for c in range(2):
            for pp in range(across):
                at = c * (blocks // 2) + pp
                extras.setdefault(at, []).append(
                    functools.partial(contract, fresh, now - 2 + c, c * 2 * CHUNK, pp)
                )
        places = [at for at in range(blocks) if at % (blocks // 2) >= across]
        pieces = [(n, pp) for n in range(per) for pp in range(across)]
        for k, (n, pp) in enumerate(pieces):
            at = places[k * len(places) // len(pieces)]
            extras.setdefault(at, []).append(functools.partial(held, per * i + n, pp))
        fill(fresh, [(now, 0), (now + 1, 2 * CHUNK)], extras)
        return 0

    lax.fori_loop(0, turns, fused, 0)
    for pp in range(POINTS // 256):
        for c in range(2):
            contract(fresh, NCHUNK - 2 + c, c * 2 * CHUNK, pp)
        for n in range(per * turns, STORED):
            held(n, pp)

    for b in range(POINTS // 128):
        t = acc[:, b * 128 : (b + 1) * 128]
        first = (t[0:4] + t[4:8]) * (1.0 / 256.0)
        second = (t[8:12] + t[12:16]) * (1.0 / 256.0)
        motion[2 * b] = jnp.where(lane4, first, pltpu.roll(second, S, axis=1))
        motion[2 * b + 1] = jnp.where(lane4, pltpu.roll(first, S, axis=1), second)

    for k in range(N_GY):
        to = lax.rem(gy + k, N_GY)
        for c in range(CAP):
            tile = motion[jnp.maximum(list_ref[c, 0, to], 0)]
            if k == 0:
                inbox[gy, c] = tile
            else:
                outbox[k, c] = tile
    for k in range(1, N_GY):
        pltpu.make_async_remote_copy(
            src_ref=outbox.at[k], dst_ref=inbox.at[gy], send_sem=ssem.at[5], recv_sem=rsem.at[5],
            device_id=(gx, lax.rem(gy + k, N_GY)), device_id_type=MESH,
        ).start()

    arrive(g3, 4)
    tiles = [g3[q] for q in range(CHIPS)]
    while len(tiles) > 1:
        tiles = [a + b for a, b in zip(tiles[::2], tiles[1::2])]
    summed = tiles[0]
    step = ratio(rr2, total(summed))
    result = x_ref[:, mine] + step * s_ref[:, mine]
    result = jnp.where(core == 0, result, pltpu.roll(result, S, axis=1))
    coef_ref[...] = result[0:3, 0:S]

    pltpu.make_async_copy(seven, seven, ssem.at[0]).wait()
    pltpu.make_async_copy(fifteen, fifteen, ssem.at[1]).wait()
    pltpu.make_async_copy(others, others, ssem.at[6]).wait()
    for buf, slot in ((g1, 2), (g2, 3), (g3, 4)):
        rest = buf.at[0 : CHIPS - 1]
        pltpu.make_async_copy(rest, rest, ssem.at[slot]).wait()

    box = inbox.at[0 : N_GY - 1]
    pltpu.make_async_copy(box, box, rsem.at[5]).wait()
    for s in range(N_GY):
        for c in range(CAP):
            tile = inbox[s, c]
            other = pltpu.roll(tile, S, axis=1)
            first = jnp.where(lane4, tile, other)
            second = jnp.where(lane4, other, tile)
            tile_ref[s * CAP + c] = first + step * second
    pltpu.make_async_copy(box, box, ssem.at[5]).wait()


WIDTH = 1024


def blend_kernel(table_ref, count_ref, tile_ref, coef_ref, out_ref, copy_ref, st, lhs):
    n = pl.program_id(0)

    @pl.when(n == 0)
    def _():
        copy_ref[...] = coef_ref[...]
        for b in range(SLOTS):
            for e in range(12):
                row = e * 12 + 3 * b
                st[row : row + 3, :] = tile_ref[table_ref[b, e]][0:3]
        lane = lax.broadcasted_iota(jnp.int32, (1, 128), 1)
        w1 = jnp.where(lane < S, lane, lane - S).astype(F32) / (S - 1)
        w0 = 1.0 - w1
        first = st[0:48, :]
        edge = first - 2.0 * (w0 * first[:, 0:1] + w1 * first[:, S - 1 : S])
        ramps = jnp.where(rows8((24, 128)) < 12, w0, w1)
        wide = jnp.concatenate([edge, ramps, jnp.zeros((8, 128), F32)], axis=0)
        high = wide.astype(BF16).astype(F32)
        stack = jnp.concatenate([high, high, wide - high, jnp.zeros((16, 128), F32)], axis=0)
        base = jnp.transpose(stack)[0:S]
        col = lax.rem(lax.rem(lax.broadcasted_iota(jnp.int32, (S, 256), 1), 80), 12)
        for b in range(SLOTS):
            alive = b < count_ref[0]
            for c in range(3):
                slot = 3 * b + c
                keep = jnp.logical_and(col == slot, alive)
                lhs[slot * S : (slot + 1) * S, :] = jnp.where(keep, base, 0.0).astype(BF16)

    spot = n * WIDTH + lax.broadcasted_iota(jnp.int32, (128, WIDTH), 1)
    cell = lax.broadcasted_iota(jnp.int32, (128, WIDTH), 0)
    pick = jnp.where(lax.shift_right_logical(spot, 6) == cell, 1.0, 0.0).astype(BF16)
    h, m, l = parts(st[48:96, :])
    spread = dot_nn(jnp.concatenate([h, m, l], axis=0).astype(BF16), pick)
    spread = spread[0:48] + spread[48:96] + spread[96:144]
    flat = n * WIDTH + lax.broadcasted_iota(jnp.int32, (8, WIDTH), 1)[0:1]
    j1 = lax.shift_right_logical(flat, 6).astype(F32) / (S - 1)
    k1 = jnp.bitwise_and(flat, 63).astype(F32) / (S - 1)
    j0 = 1.0 - j1
    k0 = 1.0 - k1
    third = jnp.concatenate([st[96:144, :]] * (WIDTH // 128), axis=1)
    sides = spread[0:24] * k0 + spread[24:48] * k1 + third[0:24] * j0 + third[24:48] * j1
    group = rows8((48, WIDTH))
    odd = jnp.logical_or(
        jnp.logical_and(group >= 12, group < 24), group >= 36
    )
    corner = jnp.where(odd, j1, j0) * jnp.where(group < 24, k0, k1)
    rh, rl = halves(jnp.concatenate([corner, sides, jnp.zeros((8, WIDTH), F32)], axis=0))
    rhs = jnp.concatenate([rh, rl, rh, jnp.zeros((16, WIDTH), BF16)], axis=0)
    full = dot_nn(lhs[...], rhs)
    for b in range(SLOTS):
        for c in range(3):
            out_ref[b, c] = full[(b * 3 + c) * S : (b * 3 + c + 1) * S]


def shards(center_points, displacements, edge_points, send_list, block_tiles, block_count):
    vmem = pl.BlockSpec(memory_space=pltpu.VMEM)
    smem = pl.BlockSpec(memory_space=pltpu.SMEM)
    coefficients, tiles = pl.pallas_call(
        motion_kernel,
        out_shape=(
            jax.ShapeDtypeStruct((3, S), F32),
            jax.ShapeDtypeStruct((N_GY * CAP, 4, 128), F32),
        ),
        in_specs=[vmem, vmem, vmem, smem],
        out_specs=(vmem, vmem),
        scratch_shapes=[
            pltpu.VMEM((N_GX, 8, 128), F32),
            pltpu.VMEM((N_GY, 4, 4, 128), F32),
            pltpu.VMEM((N_GY, 4, 4, 128), F32),
            pltpu.VMEM((CHIPS, 4, 128), F32),
            pltpu.VMEM((CHIPS, 4, 128), F32),
            pltpu.VMEM((CHIPS, 4, 128), F32),
            pltpu.VMEM((NC, 64), BF16),
            pltpu.VMEM((64, POINTS), BF16),
            pltpu.VMEM((64, 128), BF16),
            pltpu.VMEM((2 * NC, 128), BF16),
            pltpu.VMEM((POINTS // 128, STORED * 2 * CHUNK, 128), BF16),
            pltpu.VMEM((POINTS // 128, 4 * CHUNK, 128), BF16),
            pltpu.VMEM((16, POINTS), F32),
            pltpu.VMEM((16, NC), F32),
            pltpu.VMEM((16, 2 * NC), BF16),
            pltpu.VMEM((4, 8, 512), F32),
            pltpu.VMEM((4, NC), F32),
            pltpu.VMEM((4, NC), F32),
            pltpu.VMEM((4, NC), F32),
            pltpu.VMEM((4, NC), F32),
            pltpu.VMEM((EDGE_DEV, 4, 128), F32),
            pltpu.VMEM((N_GY, CAP, 4, 128), F32),
            pltpu.VMEM((N_GY, CAP, 4, 128), F32),
            pltpu.VMEM((8, POINTS), F32),
            pltpu.SemaphoreType.DMA((8,)),
            pltpu.SemaphoreType.DMA((8,)),
        ],
        compiler_params=pltpu.CompilerParams(
            collective_id=0, has_side_effects=True, vmem_limit_bytes=60 * 1024 * 1024
        ),
        name="motion",
    )(center_points, displacements, edge_points, send_list.transpose(2, 0, 1))
    block_motion, coefficients = pl.pallas_call(
        blend_kernel,
        grid=(S * S // WIDTH,),
        out_shape=(
            jax.ShapeDtypeStruct((SLOTS, 3, S, S * S), F32),
            jax.ShapeDtypeStruct((3, S), F32),
        ),
        in_specs=[smem, smem, vmem, pl.BlockSpec((3, S), lambda n: (0, 0))],
        out_specs=(
            pl.BlockSpec((SLOTS, 3, S, WIDTH), lambda n: (0, 0, 0, n)),
            pl.BlockSpec((3, S), lambda n: (0, 0)),
        ),
        scratch_shapes=[
            pltpu.VMEM((144, 128), F32),
            pltpu.VMEM((SLOTS * 3 * S, 256), BF16),
        ],
        name="blend",
    )(block_tiles, block_count, tiles, coefficients)
    return (coefficients, block_motion)


def solution(mesh):
    return jax.shard_map(
        shards,
        mesh=mesh,
        in_specs=(
            P(None, ("gx", "gy")),
            P(None, ("gx", "gy")),
            P(None, ("gx", "gy")),
            P(("gx", "gy"), None, None),
            P(("gx", "gy"), None),
            P(("gx", "gy")),
        ),
        out_specs=(P(None, ("gx", "gy")), P(("gx", "gy"), None, None, None)),
        check_vma=False,
    )
```

```python
import functools

import jax
import jax.numpy as jnp
from jax import lax
from jax.experimental import pallas as pl
from jax.experimental.pallas import tpu as pltpu
from jax.sharding import PartitionSpec as P

MESH = pl.DeviceIdType.MESH
F32 = jnp.float32
BF16 = jnp.bfloat16

NC = 8192
S = 64
SLOTS = 4
EDGE_DEV = 16
CAP = 3
N_GX = 8
N_GY = 16
CHIPS = 64
POINTS = EDGE_DEV * S
SHIFT = 0.1
CHUNK = 256
NCHUNK = NC // CHUNK
RING = (0, 1, 2, 1)


def dot_nn(left, right):
    return lax.dot_general(left, right, (((1,), (0,)), ((), ())), preferred_element_type=F32)


def dot_nt(left, right):
    return lax.dot_general(left, right, (((1,), (1,)), ((), ())), preferred_element_type=F32)


def bump(squared):
    squared = jnp.maximum(squared, 1e-30)
    root = squared * lax.rsqrt(squared)
    t = jnp.maximum(4.0 - root, 0.0)
    t2 = t * t
    return (t2 * t2) * (5.0 - t)


def halves(v):
    high = v.astype(BF16)
    return high, (v - high.astype(F32)).astype(BF16)


def parts(v):
    high = v.astype(BF16).astype(F32)
    rest = v - high
    mid = rest.astype(BF16).astype(F32)
    return high, mid, rest - mid


def rows8(shape):
    return lax.broadcasted_iota(jnp.int32, shape, 0)


def left_stack(x8):
    row = rows8(x8.shape)
    norm = jnp.sum(x8 * x8, axis=0, keepdims=True)
    v = jnp.where(row < 3, -2.0 * x8, jnp.where(row == 3, 1.0, jnp.where(row == 4, norm, 0.0)))
    h, m, l = parts(v)
    return jnp.concatenate([h, h, m, m, h, l, jnp.zeros_like(h), jnp.zeros_like(h)], axis=0)


def right_stack(x8):
    row = rows8(x8.shape)
    norm = jnp.sum(x8 * x8, axis=0, keepdims=True)
    v = jnp.where(row < 3, x8, jnp.where(row == 3, norm, jnp.where(row == 4, 1.0, 0.0)))
    h, m, l = parts(v)
    return jnp.concatenate([h, m, h, m, l, h, jnp.zeros_like(h), jnp.zeros_like(h)], axis=0)


EARLY = 6
FIRST = 10
GROUP = 5
STORED = EARLY + 2 * FIRST
TALL = 64
AHEAD = 2
OFFSETS = sorted(
    [(a, b, c) for a in range(4) for b in range(4) for c in range(4) if (a, b, c) != (0, 0, 0)],
    key=lambda o: -sum(RING[q] for q in o),
)
LINES = sorted(((a, b) for a in range(4) for b in range(4)), key=lambda o: RING[o[0]] + RING[o[1]])
NEAR = 5


def motion_kernel(
    cen_ref, dis_ref, pts_ref, list_ref, coef_ref, tile_ref,
    half, cpos, cdis, g1, g2, g3, cst, pst, ost, own_k, stored, fresh, acc, sf, sp, xs,
    d_ref, x_ref, r_ref, s_ref, motion, outbox, inbox, p8, ssem, rsem,
):
    gx = lax.axis_index("gx")
    gy = lax.axis_index("gy")
    z = lax.div(gx, 2)
    core = lax.rem(gx, 2)
    y = lax.div(gy, 4)
    x = lax.rem(gy, 4)
    me = gy * 4 + z
    lines = [lax.rem(y + a, 4) * 4 + lax.rem(x + b, 4) for a, b in LINES]

    barrier = pltpu.get_barrier_semaphore()
    for k in range(1, N_GY):
        pl.semaphore_signal(
            barrier, inc=1, device_id=(gx, lines[k]), device_id_type=MESH
        )
    for k in range(1, N_GX):
        pl.semaphore_signal(
            barrier, inc=1, device_id=(lax.rem(gx + k, N_GX), gy), device_id_type=MESH
        )

    half[gx] = jnp.zeros((8, 128), F32)
    half[gx, 0:3, 0:S] = cen_ref[...]
    half[gx, 4:7, 0:S] = dis_ref[...]
    p8[...] = jnp.zeros((8, POINTS), F32)
    p8[0:3, :] = 16.0 * (pts_ref[...] - 0.5)
    sf[...] = jnp.zeros((16, NC), F32)
    xs[...] = jnp.zeros((4, 8, 512), F32)
    for b in range(POINTS // 128):
        cols = slice(b * 128, (b + 1) * 128)
        pst[:, cols] = left_stack(p8[:, cols]).astype(BF16)
    acc[...] = jnp.zeros((16, POINTS), F32)
    fresh[...] = jnp.zeros((8, 4 * CHUNK, 128), BF16)

    pl.semaphore_wait(barrier, N_GY - 1 + N_GX - 1)

    for k in range(1, N_GX):
        pltpu.make_async_remote_copy(
            src_ref=half.at[gx], dst_ref=half.at[gx], send_sem=ssem.at[0], recv_sem=rsem.at[0],
            device_id=(lax.rem(gx + k, N_GX), gy), device_id_type=MESH,
        ).start()
    seven = half.at[0 : N_GX - 1]
    pltpu.make_async_copy(seven, seven, rsem.at[0]).wait()
    lane = lax.broadcasted_iota(jnp.int32, (8, 128), 1)
    for zz in range(4):
        both = jnp.where(lane < S, half[2 * zz], pltpu.roll(half[2 * zz + 1], S, axis=1))
        cpos[gy, zz] = both[0:4]
        cdis[gy, zz] = both[4:8]
    def to_plane(src, dst, slot, far):
        for k in range(1, N_GY):
            pltpu.make_async_remote_copy(
                src_ref=src, dst_ref=dst, send_sem=ssem.at[slot],
                recv_sem=rsem.at[slot if k < NEAR else far], device_id=(gx, lines[k]),
                device_id_type=MESH,
            ).start()

    to_plane(cpos.at[gy], cpos.at[gy], 1, 7)
    to_plane(cdis.at[gy], cdis.at[gy], 6, 6)

    def centred(t):
        return jnp.where(rows8(t.shape) < 3, 16.0 * (t - 0.5), 0.0)

    def build(k):
        line = lines[k]
        rows = slice(k * 512, k * 512 + 512)
        xs[k % 4, 0:4, :] = centred(jnp.concatenate([cpos[line, zz] for zz in range(4)], axis=1))
        cst[rows, :] = jnp.transpose(right_stack(xs[k % 4])).astype(BF16)

    def fill_own(n, _):
        rows = pl.ds(pl.multiple_of(n * CHUNK, CHUNK), CHUNK)
        base = pl.multiple_of(n * (2 * CHUNK), 2 * CHUNK)
        high, low = halves(bump(dot_nn(cst[rows, :], ost[...])))
        own_k[pl.ds(base, CHUNK), :] = high
        own_k[pl.ds(base + CHUNK, CHUNK), :] = low
        return 0

    def fill(dst, jobs, extras):
        blocks = [
            (n, base, jb, pp)
            for n, base in jobs
            for jb in range(CHUNK // TALL)
            for pp in range(POINTS // 256)
        ]

        def distance(block):
            n, _, jb, pp = block
            start = n * CHUNK + jb * TALL
            rows = pl.ds(start if isinstance(n, int) else pl.multiple_of(start, TALL), TALL)
            return dot_nn(cst[rows, :], pst[:, pp * 256 : (pp + 1) * 256])

        ready = [distance(block) for block in blocks[:AHEAD]]
        for at, (n, base, jb, pp) in enumerate(blocks):
            if at + AHEAD < len(blocks):
                ready.append(distance(blocks[at + AHEAD]))
            for extra in extras.get(at, ()):
                extra()
            high, low = halves(bump(ready.pop(0)))
            for half_at in range(2):
                part = slice(half_at * 128, half_at * 128 + 128)
                dst[2 * pp + half_at, pl.ds(base + jb * TALL, TALL), :] = high[:, part]
                dst[2 * pp + half_at, pl.ds(base + CHUNK + jb * TALL, TALL), :] = low[:, part]

    def fill_stored(first, count):
        def turn(i, _):
            n = first + i * GROUP
            fill(stored, [(n + k, row_of(n + k)) for k in range(GROUP)], {})
            return 0

        def row_of(n):
            return pl.multiple_of(n * (2 * CHUNK), 2 * CHUNK)

        whole = count // GROUP
        if whole:
            lax.fori_loop(0, whole, turn, 0)
        for n in range(first + whole * GROUP, first + count):
            fill(stored, [(n, n * 2 * CHUNK)], {})

    build(0)
    p8[:, 0:128] = jnp.zeros((8, 128), F32)
    p8[0:4, 0:128] = centred(cpos[gy, z])
    ost[...] = left_stack(p8[:, 0:128]).astype(BF16)
    lax.fori_loop(0, 2, fill_own, 0)
    fill_stored(0, 2)

    near = cpos.at[0 : NEAR - 1]
    pltpu.make_async_copy(near, near, rsem.at[1]).wait()
    for k in range(1, NEAR):
        build(k)
    lax.fori_loop(2, 2 * NEAR, fill_own, 0, unroll=4)
    fill_stored(2, EARLY - 2)

    far = cpos.at[0 : N_GY - NEAR]
    pltpu.make_async_copy(far, far, rsem.at[7]).wait()
    for k in range(NEAR, N_GY):
        build(k)
    lax.fori_loop(2 * NEAR, NCHUNK, fill_own, 0, unroll=2)
    fifteen = cpos.at[0 : N_GY - 1]
    others = cdis.at[0 : N_GY - 1]
    pltpu.make_async_copy(others, others, rsem.at[6]).wait()
    order = [(line, zz) for line in lines for zz in range(4)]
    d_ref[...] = jnp.concatenate([cdis[line, zz] for line, zz in order], axis=1)

    def set_search(search):
        high = search.astype(BF16).astype(F32)
        sf[8:12, :] = high
        sf[12:16, :] = search - high

    def apply_own():
        for n in range(NCHUNK):
            value = sf[:, n * CHUNK : (n + 1) * CHUNK].astype(BF16)
            sp[:, 2 * n * CHUNK : (2 * n + 1) * CHUNK] = value
            sp[:, (2 * n + 1) * CHUNK : (2 * n + 2) * CHUNK] = value
        t = dot_nn(sp[...], own_k[...])
        return (t[8:12] + t[12:16]) * (1.0 / 256.0)

    def spread(buf, slot):
        for a, b, c in OFFSETS:
            zz = lax.rem(z + a, 4)
            to = (2 * zz + core, lax.rem(y + b, 4) * 4 + lax.rem(x + c, 4))
            pltpu.make_async_remote_copy(
                src_ref=buf.at[me], dst_ref=buf.at[me], send_sem=ssem.at[slot],
                recv_sem=rsem.at[slot], device_id=to, device_id_type=MESH,
            ).start()

    def arrive(buf, slot):
        rest = buf.at[0 : CHIPS - 1]
        pltpu.make_async_copy(rest, rest, rsem.at[slot]).wait()

    def collected(buf):
        return jnp.concatenate([buf[line * 4 + zz] for line, zz in order], axis=1)

    def total(v):
        return jnp.sum(v, axis=1, keepdims=True)

    live = lax.broadcasted_iota(jnp.int32, (4, 1), 0) < 3

    def ratio(top, bottom):
        return top / jnp.where(live, bottom, 1.0)

    set_search(d_ref[...])
    g1[me] = apply_own()
    spread(g1, 2)
    fill_stored(EARLY, FIRST)
    arrive(g1, 2)
    d = d_ref[...]
    rr0 = total(d * d)
    applied = collected(g1) + SHIFT * d
    step = ratio(rr0, total(d * applied))
    remain = d - step * applied
    rr1 = total(remain * remain)
    search = remain + ratio(rr1, rr0) * d
    x_ref[...] = step * d
    r_ref[...] = remain
    s_ref[...] = search

    set_search(search)
    g2[me] = apply_own()
    spread(g2, 3)
    fill_stored(EARLY + FIRST, FIRST)
    arrive(g2, 3)
    search = s_ref[...]
    applied = collected(g2) + SHIFT * search
    step = ratio(rr1, total(search * applied))
    iterate = x_ref[...] + step * search
    remain = r_ref[...] - step * applied
    rr2 = total(remain * remain)
    search = remain + ratio(rr2, rr1) * search
    x_ref[...] = iterate
    s_ref[...] = search
    set_search(search)
    high = iterate.astype(BF16).astype(F32)
    sf[0:4, :] = high
    sf[4:8, :] = iterate - high

    mine = pl.ds(pl.multiple_of(z * 128, 128), 128)
    last = apply_own()
    own_search = s_ref[:, mine]
    g3[me] = own_search * (last + SHIFT * own_search)
    spread(g3, 4)

    lane4 = lax.broadcasted_iota(jnp.int32, (4, 128), 1) < S

    def at_chunk(n):
        return n * 2 * CHUNK if isinstance(n, int) else pl.multiple_of(n * (2 * CHUNK), 2 * CHUNK)

    def contract(src, n, base, pp):
        lhs = sp[:, pl.ds(at_chunk(n), 2 * CHUNK)]
        rows = pl.ds(base, 2 * CHUNK)
        cols = slice(pp * 256, (pp + 1) * 256)
        rhs = jnp.concatenate([src[2 * pp, rows, :], src[2 * pp + 1, rows, :]], axis=1)
        acc[:, cols] += dot_nn(lhs, rhs)

    def held(n, pp):
        contract(stored, n, at_chunk(n), pp)

    turns = (NCHUNK - STORED) // 2
    per = STORED // turns

    def fused(i, _):
        now = STORED + 2 * i
        across = POINTS // 256
        blocks = 2 * (CHUNK // TALL) * across
        extras = {}
        for c in range(2):
            for pp in range(across):
                at = c * (blocks // 2) + pp
                extras.setdefault(at, []).append(
                    functools.partial(contract, fresh, now - 2 + c, c * 2 * CHUNK, pp)
                )
        places = [at for at in range(blocks) if at % (blocks // 2) >= across]
        pieces = [(n, pp) for n in range(per) for pp in range(across)]
        for k, (n, pp) in enumerate(pieces):
            at = places[k * len(places) // len(pieces)]
            extras.setdefault(at, []).append(functools.partial(held, per * i + n, pp))
        fill(fresh, [(now, 0), (now + 1, 2 * CHUNK)], extras)
        return 0

    lax.fori_loop(0, turns, fused, 0)
    for pp in range(POINTS // 256):
        for c in range(2):
            contract(fresh, NCHUNK - 2 + c, c * 2 * CHUNK, pp)
        for n in range(per * turns, STORED):
            held(n, pp)

    for b in range(POINTS // 128):
        t = acc[:, b * 128 : (b + 1) * 128]
        first = (t[0:4] + t[4:8]) * (1.0 / 256.0)
        second = (t[8:12] + t[12:16]) * (1.0 / 256.0)
        motion[2 * b] = jnp.where(lane4, first, pltpu.roll(second, S, axis=1))
        motion[2 * b + 1] = jnp.where(lane4, pltpu.roll(first, S, axis=1), second)

    for k in reversed(range(N_GY)):
        to = lines[k]
        for c in range(CAP):
            tile = motion[jnp.maximum(list_ref[c, 0, to], 0)]
            if k == 0:
                inbox[gy, c] = tile
            else:
                outbox[k, c] = tile
    for k in reversed(range(1, N_GY)):
        pltpu.make_async_remote_copy(
            src_ref=outbox.at[k], dst_ref=inbox.at[gy], send_sem=ssem.at[5], recv_sem=rsem.at[5],
            device_id=(gx, lines[k]), device_id_type=MESH,
        ).start()

    arrive(g3, 4)
    tiles = [g3[q] for q in range(CHIPS)]
    while len(tiles) > 1:
        tiles = [a + b for a, b in zip(tiles[::2], tiles[1::2])]
    summed = tiles[0]
    step = ratio(rr2, total(summed))
    result = x_ref[:, mine] + step * s_ref[:, mine]
    result = jnp.where(core == 0, result, pltpu.roll(result, S, axis=1))
    coef_ref[...] = result[0:3, 0:S]

    pltpu.make_async_copy(seven, seven, ssem.at[0]).wait()
    pltpu.make_async_copy(fifteen, fifteen, ssem.at[1]).wait()
    pltpu.make_async_copy(others, others, ssem.at[6]).wait()
    for buf, slot in ((g1, 2), (g2, 3), (g3, 4)):
        rest = buf.at[0 : CHIPS - 1]
        pltpu.make_async_copy(rest, rest, ssem.at[slot]).wait()

    box = inbox.at[0 : N_GY - 1]
    pltpu.make_async_copy(box, box, rsem.at[5]).wait()
    for s in range(N_GY):
        for c in range(CAP):
            tile = inbox[s, c]
            other = pltpu.roll(tile, S, axis=1)
            first = jnp.where(lane4, tile, other)
            second = jnp.where(lane4, other, tile)
            tile_ref[s * CAP + c] = first + step * second
    pltpu.make_async_copy(box, box, ssem.at[5]).wait()


WIDTH = 1024


def blend_kernel(table_ref, count_ref, tile_ref, coef_ref, out_ref, copy_ref, st, lhs):
    n = pl.program_id(0)

    @pl.when(n == 0)
    def _():
        copy_ref[...] = coef_ref[...]
        for b in range(SLOTS):
            for e in range(12):
                row = e * 12 + 3 * b
                st[row : row + 3, :] = tile_ref[table_ref[b, e]][0:3]
        lane = lax.broadcasted_iota(jnp.int32, (1, 128), 1)
        w1 = jnp.where(lane < S, lane, lane - S).astype(F32) / (S - 1)
        w0 = 1.0 - w1
        first = st[0:48, :]
        edge = first - 2.0 * (w0 * first[:, 0:1] + w1 * first[:, S - 1 : S])
        ramps = jnp.where(rows8((24, 128)) < 12, w0, w1)
        wide = jnp.concatenate([edge, ramps, jnp.zeros((8, 128), F32)], axis=0)
        high = wide.astype(BF16).astype(F32)
        stack = jnp.concatenate([high, high, wide - high, jnp.zeros((16, 128), F32)], axis=0)
        base = jnp.transpose(stack)[0:S]
        col = lax.rem(lax.rem(lax.broadcasted_iota(jnp.int32, (S, 256), 1), 80), 12)
        for b in range(SLOTS):
            alive = b < count_ref[0]
            for c in range(3):
                slot = 3 * b + c
                keep = jnp.logical_and(col == slot, alive)
                lhs[slot * S : (slot + 1) * S, :] = jnp.where(keep, base, 0.0).astype(BF16)

    spot = n * WIDTH + lax.broadcasted_iota(jnp.int32, (128, WIDTH), 1)
    cell = lax.broadcasted_iota(jnp.int32, (128, WIDTH), 0)
    pick = jnp.where(lax.shift_right_logical(spot, 6) == cell, 1.0, 0.0).astype(BF16)
    h, m, l = parts(st[48:96, :])
    spread = dot_nn(jnp.concatenate([h, m, l], axis=0).astype(BF16), pick)
    spread = spread[0:48] + spread[48:96] + spread[96:144]
    flat = n * WIDTH + lax.broadcasted_iota(jnp.int32, (8, WIDTH), 1)[0:1]
    j1 = lax.shift_right_logical(flat, 6).astype(F32) / (S - 1)
    k1 = jnp.bitwise_and(flat, 63).astype(F32) / (S - 1)
    j0 = 1.0 - j1
    k0 = 1.0 - k1
    third = jnp.concatenate([st[96:144, :]] * (WIDTH // 128), axis=1)
    sides = spread[0:24] * k0 + spread[24:48] * k1 + third[0:24] * j0 + third[24:48] * j1
    group = rows8((48, WIDTH))
    odd = jnp.logical_or(
        jnp.logical_and(group >= 12, group < 24), group >= 36
    )
    corner = jnp.where(odd, j1, j0) * jnp.where(group < 24, k0, k1)
    rh, rl = halves(jnp.concatenate([corner, sides, jnp.zeros((8, WIDTH), F32)], axis=0))
    rhs = jnp.concatenate([rh, rl, rh, jnp.zeros((16, WIDTH), BF16)], axis=0)
    full = dot_nn(lhs[...], rhs)
    for b in range(SLOTS):
        for c in range(3):
            out_ref[b, c] = full[(b * 3 + c) * S : (b * 3 + c + 1) * S]


def shards(center_points, displacements, edge_points, send_list, block_tiles, block_count):
    vmem = pl.BlockSpec(memory_space=pltpu.VMEM)
    smem = pl.BlockSpec(memory_space=pltpu.SMEM)
    coefficients, tiles = pl.pallas_call(
        motion_kernel,
        out_shape=(
            jax.ShapeDtypeStruct((3, S), F32),
            jax.ShapeDtypeStruct((N_GY * CAP, 4, 128), F32),
        ),
        in_specs=[vmem, vmem, vmem, smem],
        out_specs=(vmem, vmem),
        scratch_shapes=[
            pltpu.VMEM((N_GX, 8, 128), F32),
            pltpu.VMEM((N_GY, 4, 4, 128), F32),
            pltpu.VMEM((N_GY, 4, 4, 128), F32),
            pltpu.VMEM((CHIPS, 4, 128), F32),
            pltpu.VMEM((CHIPS, 4, 128), F32),
            pltpu.VMEM((CHIPS, 4, 128), F32),
            pltpu.VMEM((NC, 64), BF16),
            pltpu.VMEM((64, POINTS), BF16),
            pltpu.VMEM((64, 128), BF16),
            pltpu.VMEM((2 * NC, 128), BF16),
            pltpu.VMEM((POINTS // 128, STORED * 2 * CHUNK, 128), BF16),
            pltpu.VMEM((POINTS // 128, 4 * CHUNK, 128), BF16),
            pltpu.VMEM((16, POINTS), F32),
            pltpu.VMEM((16, NC), F32),
            pltpu.VMEM((16, 2 * NC), BF16),
            pltpu.VMEM((4, 8, 512), F32),
            pltpu.VMEM((4, NC), F32),
            pltpu.VMEM((4, NC), F32),
            pltpu.VMEM((4, NC), F32),
            pltpu.VMEM((4, NC), F32),
            pltpu.VMEM((EDGE_DEV, 4, 128), F32),
            pltpu.VMEM((N_GY, CAP, 4, 128), F32),
            pltpu.VMEM((N_GY, CAP, 4, 128), F32),
            pltpu.VMEM((8, POINTS), F32),
            pltpu.SemaphoreType.DMA((8,)),
            pltpu.SemaphoreType.DMA((8,)),
        ],
        compiler_params=pltpu.CompilerParams(
            collective_id=0, has_side_effects=True, vmem_limit_bytes=60 * 1024 * 1024
        ),
        name="motion",
    )(center_points, displacements, edge_points, send_list.transpose(2, 0, 1))
    block_motion, coefficients = pl.pallas_call(
        blend_kernel,
        grid=(S * S // WIDTH,),
        out_shape=(
            jax.ShapeDtypeStruct((SLOTS, 3, S, S * S), F32),
            jax.ShapeDtypeStruct((3, S), F32),
        ),
        in_specs=[smem, smem, vmem, pl.BlockSpec((3, S), lambda n: (0, 0))],
        out_specs=(
            pl.BlockSpec((SLOTS, 3, S, WIDTH), lambda n: (0, 0, 0, n)),
            pl.BlockSpec((3, S), lambda n: (0, 0)),
        ),
        scratch_shapes=[
            pltpu.VMEM((144, 128), F32),
            pltpu.VMEM((SLOTS * 3 * S, 256), BF16),
        ],
        name="blend",
    )(block_tiles, block_count, tiles, coefficients)
    return (coefficients, block_motion)


def solution(mesh):
    return jax.shard_map(
        shards,
        mesh=mesh,
        in_specs=(
            P(None, ("gx", "gy")),
            P(None, ("gx", "gy")),
            P(None, ("gx", "gy")),
            P(("gx", "gy"), None, None),
            P(("gx", "gy"), None),
            P(("gx", "gy")),
        ),
        out_specs=(P(None, ("gx", "gy")), P(("gx", "gy"), None, None, None)),
        check_vma=False,
    )
```
